1024 devices in a mesh: dp: 128 (over y, z, core), tensor: 8 (over x).
Axes of the slice: x: 8, y: 8, z: 8, core: 2. Of those that a mesh axis runs over, the one named last changes fastest.
Arguments:
- activations: bfloat16 [32768, 3072], P('dp'), may hold values from -6 to 6
- basis_init: float32 [3, 1024, 64], P(None, 'tensor'), may hold values from -6 to 6
- owner_table: int32 [3], replicated, may hold values from 1 to 64, as said below
Outputs:
- covariance: float32 [3, 1024, 1024], P(None, 'tensor', 'dp')
- basis: float32 [3, 1024, 64], P(None, 'tensor')
- eigen: float32 [3, 64], replicated
- owned_eigen: float32 [256, 64], P('dp')
The draws below stay inside these ranges and needn't reach their ends.
Inputs may be any that keep to these rules, and one draw needn't show every extreme that they name: `owner_table`: the owners are index 1 and index 64 of dp; one of them owns exactly 2 blocks, the other the rest.
All inputs are finite; a program needn't handle non-finite values.
Results may differ from the reference program's by a relative error of at most 0.0003.
Values sent between devices are 32-bit elements; how exact they have to be, the bound alone decides.
No kernel may reach another device: no remote copies, remote signals or barrier semaphores. Data moves between devices by JAX's collectives and lax.ppermute only.
A program may use at most 32 MiB of HBM per device.

```python
import jax
import jax.numpy as jnp
from jax import lax

NB = 3
BO = 1024
K = 64
CAP = 2
ITERS = 2
TOKENS = 32768
N_DP = 128


def draw_owner_table(key, part):
    first_key, second_key = jax.random.split(jax.random.fold_in(key, 7), 2)
    flipped = jax.random.randint(first_key, (), 0, 2)
    busiest = jnp.where(flipped == 1, N_DP // 2, 1)
    lighter = jnp.where(flipped == 1, 1, N_DP // 2)
    shuffled = jax.random.permutation(second_key, NB)
    heavy = shuffled < CAP
    return jnp.where(heavy, busiest, lighter).astype(jnp.int32)


def shard_levels(own_key, dims, pieces, least, top_value):
    gain, own = 1.0, jax.random.fold_in(own_key, 6)
    for axis_at, parts in pieces:
        draws = jnp.exp(jax.random.uniform(jax.random.fold_in(own, axis_at), (parts,), jnp.float32, least / len(pieces), top_value / len(pieces)))
        gain = gain * jnp.repeat(draws, dims[axis_at] // parts).reshape([-1 if axis == axis_at else 1 for axis in range(len(dims))])
    return gain


def normal_values(own_key, dims, scale, limit, cuts=(), dtype=jnp.bfloat16):
    array = jax.random.normal(own_key, dims, jnp.float32) * scale
    if len(cuts) > 0:
        array = shard_levels(own_key, dims, cuts, -0.22, 0.18) * array
    return jnp.clip(array, min=-limit, max=limit).astype(dtype)


def setup_inputs(seed: int = 0) -> dict:
    arg_keys = jax.random.split(jax.random.key(seed), 4)
    activations = normal_values(arg_keys[0], (TOKENS, NB * BO), 1.0, 6.0, ((0, 128),))
    basis_init = normal_values(arg_keys[1], (NB, BO, K), 1.0, 6.0, ((1, 8),), jnp.float32)
    owner_table = draw_owner_table(jax.random.fold_in(arg_keys[3], 71), 0)
    return dict(activations=activations, basis_init=basis_init, owner_table=owner_table)


def reference(activations, basis_init, owner_table):
    highest = lax.Precision.HIGHEST
    cov_list = []
    basis_list = []
    eigen_list = []
    for block_id in range(NB):
        columns = activations[:, block_id * BO:(block_id + 1) * BO]
        covariance = jnp.dot(columns.T.astype(jnp.float32), columns.astype(jnp.float32), preferred_element_type=jnp.float32) / TOKENS
        cov_list.append(covariance)
        current = basis_init[block_id]
        diagonal_part = jnp.zeros((K,), jnp.float32)
        for iteration in range(ITERS):
            image = jnp.dot(covariance, current, precision=highest)
            gram = jnp.dot(image.T, image, precision=highest)
            lower = jnp.linalg.cholesky(gram)
            current = lax.linalg.triangular_solve(lower, image, left_side=False, lower=True, transpose_a=True)
            diagonal_part = jnp.diagonal(lower)
        basis_list.append(current * jnp.sqrt(jnp.float32(BO)))
        eigen_list.append(diagonal_part)
    covariance_all = jnp.stack(cov_list)
    basis = jnp.stack(basis_list)
    eigen = jnp.stack(eigen_list)
    positions = jnp.arange(NB).astype(jnp.int32)
    earlier = (owner_table[:, None] == owner_table[None, :]) & (positions[None, :] < positions[:, None])
    slot_of = lax.optimization_barrier(jnp.sum(earlier.astype(jnp.int32), axis=1)).astype(jnp.int32)
    target = (owner_table * CAP + slot_of).astype(jnp.int32)
    owned_eigen = jnp.zeros((N_DP * CAP, K), jnp.float32).at[target].set(eigen)
    return (covariance_all, basis, eigen, owned_eigen)
```

```python
import functools
import math

import jax
import jax.numpy as jnp
from jax import lax
from jax.experimental import pallas as pl
from jax.experimental.pallas import tpu as pltpu
from jax.sharding import PartitionSpec as P

CAP = 2
HIGHEST = lax.Precision.HIGHEST
SMALL = pltpu.CompilerParams(vmem_limit_bytes=16 << 20)


def product(a, b, contract_b):
    dims = (((1,), (contract_b,)), ((), ()))
    return lax.dot_general(a, b, dims, precision=HIGHEST, preferred_element_type=jnp.float32)


def product_rows(a, b):
    dims = (((0,), (0,)), ((), ()))
    return lax.dot_general(a, b, dims, precision=HIGHEST, preferred_element_type=jnp.float32)


def packed(gram):
    half = gram.shape[0] // 2
    return jnp.concatenate([gram[:half], gram[half:]], axis=1)


def unpacked(rows):
    half = rows.shape[1] // 2
    return jnp.concatenate([rows[:, :half], rows[:, half:]], axis=0)


def factor(grams):
    order = grams[0].shape[0]
    groups = order // 8
    sub = lax.broadcasted_iota(jnp.int32, (8, 2 * order), 0)
    row_at = lax.broadcasted_iota(jnp.int32, (order, order), 0)
    col_at = lax.broadcasted_iota(jnp.int32, (order, order), 1)
    identity = (row_at == col_at).astype(jnp.float32)
    tiles = []
    for gram in grams:
        both = jnp.concatenate([gram, identity], axis=1)
        tiles.append([both[8 * g : 8 * g + 8] for g in range(groups)])
    for pivot in range(order):
        group, place = divmod(pivot, 8)
        for held in tiles:
            row = held[group][place : place + 1]
            square = row[:, pivot : pivot + 1]
            inverse = lax.rsqrt(square)
            inverse = inverse * (1.5 - 0.5 * ((square * inverse) * inverse))
            row = row * inverse
            for g in range(group, groups):
                reduced = held[g] - (held[g][:, pivot : pivot + 1] * inverse) * row
                if g == group:
                    reduced = jnp.where(sub > place, reduced, jnp.where(sub == place, row, held[g]))
                held[g] = reduced
    results = []
    for held in tiles:
        both = jnp.concatenate(held, axis=0)
        diagonal = jnp.sum(both[:, :order] * identity, axis=0, keepdims=True)
        results.append((both[:, order:], diagonal))
    return results


def cov_kernel(scale, at_ref, slab_ref, columns_ref, keep_ref, send_ref):
    dims = (((0,), (0,)), ((), ()))
    term = lax.dot_general(columns_ref[...], slab_ref[...], dims, preferred_element_type=jnp.float32)
    pairs, _, share, rows = keep_ref.shape
    term = (term * scale).reshape(pairs, 2, share, rows)
    first = at_ref[1] == 0
    keep_ref[:, 0] = jnp.where(first, term[:, 0], term[:, 1])
    send_ref[:, 0] = jnp.where(first, term[:, 1], term[:, 0])


def piece_kernel(pieces_ref, basis_ref, own_ref, part_ref):
    blocks, share, _ = own_ref.shape
    vectors = basis_ref.shape[1]
    part_ref[...] = jnp.zeros(part_ref.shape, jnp.float32)
    for b in range(blocks):
        own = jnp.sum(pieces_ref[:, b], axis=0)
        own_ref[b] = own
        part_ref[:, b * vectors : (b + 1) * vectors] = product(own, basis_ref[b], 1)


def image_kernel(parts_ref, own_ref, out_ref):
    blocks = own_ref.shape[0]
    vectors = out_ref.shape[1] * 2 // 3
    images = parts_ref[0]
    for t in range(1, parts_ref.shape[0]):
        images = images + parts_ref[t]
    for b in range(blocks):
        image = images[:, b * vectors : (b + 1) * vectors]
        out_ref[b, :vectors] = product_rows(image, own_ref[b])
        out_ref[b, vectors:] = packed(product_rows(image, image))


def first_kernel(sums_ref, next_ref, gram_ref):
    blocks, vectors, _ = next_ref.shape
    factors = factor([unpacked(sums_ref[b, vectors:]) for b in range(blocks)])
    for b in range(blocks):
        image = product(factors[b][0], sums_ref[b, :vectors], 0)
        next_ref[b] = image
        gram_ref[b] = packed(product(image, image, 1))


def second_kernel(image_ref, grams_ref, basis_ref, eigen_ref):
    blocks = image_ref.shape[0]
    root_scale = math.sqrt(grams_ref.shape[0] * image_ref.shape[2])
    grams = []
    for b in range(blocks):
        gram = grams_ref[0, b]
        for t in range(1, grams_ref.shape[0]):
            gram = gram + grams_ref[t, b]
        grams.append(unpacked(gram))
    factors = factor(grams)
    for b in range(blocks):
        basis_ref[b] = product(factors[b][0], image_ref[b], 0) * root_scale
        eigen_ref[b : b + 1] = factors[b][1]


def copies(x, n):
    return jnp.broadcast_to(x[None], (n,) + x.shape)


def f32(*dims):
    return jax.ShapeDtypeStruct(dims, jnp.float32)


def body(activations, basis_init, owner_table):
    dp_count = lax.axis_size("dp")
    tp_count = lax.axis_size("tensor")
    dp_index = lax.axis_index("dp")
    tp_index = lax.axis_index("tensor")
    tok_rows = activations.shape[0]
    blocks, slab_rows, vectors = basis_init.shape
    order_size = activations.shape[1] // blocks
    share = order_size // dp_count
    pairs = dp_count // 2

    halves = pl.BlockSpec((pairs, 1, share, slab_rows), lambda b, at: (0, b, 0, 0))
    keep, send = pl.pallas_call(
        functools.partial(cov_kernel, 1.0 / (tok_rows * dp_count)),
        grid_spec=pltpu.PrefetchScalarGridSpec(
            num_scalar_prefetch=1,
            grid=(blocks,),
            in_specs=[
                pl.BlockSpec((tok_rows, slab_rows), lambda b, at: (0, b * tp_count + at[0])),
                pl.BlockSpec((tok_rows, order_size), lambda b, at: (0, b)),
            ],
            out_specs=(halves, halves),
        ),
        out_shape=(f32(pairs, blocks, share, slab_rows),) * 2,
        name="cov",
        compiler_params=SMALL,
    )(jnp.stack([tp_index, dp_index % 2]), activations, activations)
    partner = lax.ppermute(send, "dp", [(i, i ^ 1) for i in range(dp_count)])
    same_core = [list(range(core, dp_count, 2)) for core in range(2)]
    pieces = lax.all_to_all(keep + partner, "dp", 0, 0, axis_index_groups=same_core)
    lanes = -(-blocks * vectors // 128) * 128
    own, part = pl.pallas_call(
        piece_kernel, out_shape=(f32(blocks, share, slab_rows), f32(share, lanes)), name="piece", compiler_params=SMALL
    )(pieces, jnp.swapaxes(basis_init, 1, 2))

    parts = lax.all_to_all(copies(part, tp_count), "tensor", 0, 0)
    height = vectors + vectors // 2
    terms = pl.pallas_call(image_kernel, out_shape=f32(blocks, height, slab_rows), name="image", compiler_params=SMALL)(parts, own)
    rows = blocks * height
    each = -(-rows // dp_count)
    terms = terms.reshape(rows, slab_rows)
    terms = jnp.concatenate([terms, jnp.zeros((each * dp_count - rows, slab_rows), jnp.float32)], axis=0)
    terms = lax.all_to_all(terms.reshape(dp_count, each * slab_rows), "dp", 0, 0)
    terms = jnp.sum(terms, axis=0)
    sums = lax.all_to_all(copies(terms, dp_count), "dp", 0, 0)
    sums = sums.reshape(each * dp_count, slab_rows)[:rows].reshape(blocks, height, slab_rows)

    image, gram = pl.pallas_call(
        first_kernel, out_shape=(f32(blocks, vectors, slab_rows), f32(blocks, vectors // 2, 2 * vectors)), name="first", compiler_params=SMALL
    )(sums)
    grams = lax.all_to_all(copies(gram, tp_count), "tensor", 0, 0)
    basis, eigen = pl.pallas_call(
        second_kernel, out_shape=(f32(blocks, vectors, slab_rows), f32(blocks, vectors)), name="second", compiler_params=SMALL
    )(image, grams)

    positions = jnp.arange(blocks)
    earlier = (owner_table[:, None] == owner_table[None, :]) & (positions[None, :] < positions[:, None])
    slot_of = jnp.sum(earlier.astype(jnp.int32), axis=1)
    table_match = (owner_table[None, :] == dp_index) & (slot_of[None, :] == jnp.arange(CAP)[:, None])
    owned_eigen = jnp.sum(jnp.where(table_match[:, :, None], eigen[None], 0.0), axis=1)
    return (jnp.swapaxes(own, 1, 2), jnp.swapaxes(basis, 1, 2), eigen, owned_eigen)


def solution(mesh):
    return jax.shard_map(
        body,
        mesh=mesh,
        in_specs=(P("dp", None), P(None, "tensor", None), P()),
        out_specs=(P(None, "tensor", "dp"), P(None, "tensor", None), P(), P("dp", None)),
        check_vma=False,
    )
```

```python
import functools
import math

import jax
import jax.numpy as jnp
from jax import lax
from jax.experimental import pallas as pl
from jax.experimental.pallas import tpu as pltpu
from jax.sharding import PartitionSpec as P

CAP = 2
HIGHEST = lax.Precision.HIGHEST
SMALL = pltpu.CompilerParams(vmem_limit_bytes=16 << 20)


def product(a, b, contract_b):
    dims = (((1,), (contract_b,)), ((), ()))
    return lax.dot_general(a, b, dims, precision=HIGHEST, preferred_element_type=jnp.float32)


def product_rows(a, b):
    dims = (((0,), (0,)), ((), ()))
    return lax.dot_general(a, b, dims, precision=HIGHEST, preferred_element_type=jnp.float32)


def packed(gram):
    half = gram.shape[0] // 2
    return jnp.concatenate([gram[:half], gram[half:]], axis=1)


def unpacked(rows):
    half = rows.shape[1] // 2
    return jnp.concatenate([rows[:, :half], rows[:, half:]], axis=0)


def quadrants(gram):
    half = gram.shape[0] // 2
    quads = (gram[:half, :half], gram[half:, :half], gram[half:, half:])
    return jnp.concatenate([jnp.concatenate([q[r : r + 8] for r in range(0, half, 8)], axis=1) for q in quads], axis=0)


def whole_gram(rows, order):
    half = order // 2
    quads = []
    for q in range(3):
        part = rows[q * 8 : q * 8 + 8]
        quads.append(jnp.concatenate([part[:, c : c + half] for c in range(0, part.shape[1], half)], axis=0))
    upper = jnp.concatenate([quads[0], quads[1].T], axis=1)
    lower = jnp.concatenate([quads[1], quads[2]], axis=1)
    return jnp.concatenate([upper, lower], axis=0)


def refined_rsqrt(x):
    r = lax.rsqrt(x)
    return r * (1.5 - 0.5 * ((x * r) * r))


def factor(grams):
    order = grams[0].shape[0]
    groups = order // 8
    wide = 2 * order
    sub = lax.broadcasted_iota(jnp.int32, (8, wide), 0)
    lane = lax.broadcasted_iota(jnp.int32, (8, wide), 1)
    row_at = lax.broadcasted_iota(jnp.int32, (order, order), 0)
    col_at = lax.broadcasted_iota(jnp.int32, (order, order), 1)
    identity = (row_at == col_at).astype(jnp.float32)

    def full(x):
        return jnp.broadcast_to(x, (8, wide))

    tiles = []
    for gram in grams:
        both = jnp.concatenate([gram, identity], axis=1)
        tiles.append([both[8 * g : 8 * g + 8] for g in range(groups)])
    for pivot in range(order):
        group, place = divmod(pivot, 8)
        for held in tiles:
            own = full(held[group][:, pivot : pivot + 1])
            scaled = full(held[group][place : place + 1]) * (1.0 / full(own[place : place + 1]))
            for g in range(group, groups):
                if g == group and place == 7:
                    continue
                column = own if g == group else full(held[g][:, pivot : pivot + 1])
                reduced = held[g] - column * scaled
                held[g] = jnp.where(sub > place, reduced, held[g]) if g == group else reduced
    results = []
    for held in tiles:
        rows = []
        for g in range(groups):
            square = jnp.sum(jnp.where(lane == sub + 8 * g, held[g], 0.0), axis=1, keepdims=True)
            rows.append(held[g] * refined_rsqrt(square))
        both = jnp.concatenate(rows, axis=0)
        results.append((both[:, order:], jnp.sum(both[:, :order] * identity, axis=0, keepdims=True)))
    return results


def cov_kernel(scale, at_ref, core_ref, slab_ref, columns_ref, keep_ref, send_ref):
    dims = (((0,), (0,)), ((), ()))
    term = lax.dot_general(columns_ref[...], slab_ref[...], dims, preferred_element_type=jnp.float32)
    pairs, _, share, rows = keep_ref.shape
    term = (term * scale).reshape(pairs, 2, share, rows)
    first = core_ref[0] == 0
    keep_ref[:, 0] = jnp.where(first, term[:, 0], term[:, 1])
    send_ref[:, 0] = jnp.where(first, term[:, 1], term[:, 0])


def piece_kernel(pieces_ref, basis_ref, out_ref, own_ref, part_ref):
    blocks, share, _ = own_ref.shape
    vectors = basis_ref.shape[1]
    part_ref[...] = jnp.zeros(part_ref.shape, jnp.float32)
    for b in range(blocks):
        own = jnp.sum(pieces_ref[:, b], axis=0)
        out_ref[b] = own
        own_ref[b] = own
        part_ref[:, b * vectors : (b + 1) * vectors] = product(own, basis_ref[b], 1)


def image_kernel(vectors, parts_ref, own_ref, out_ref):
    blocks = own_ref.shape[0]
    height = vectors + vectors // 2
    images = parts_ref[0]
    for t in range(1, parts_ref.shape[0]):
        images = images + parts_ref[t]
    for b in range(blocks):
        image = images[:, b * vectors : (b + 1) * vectors]
        out_ref[b * height : b * height + vectors] = product_rows(image, own_ref[b])
        out_ref[b * height + vectors : (b + 1) * height] = packed(product_rows(image, image))
    rest = out_ref.shape[0] - blocks * height
    if rest > 0:
        out_ref[blocks * height :] = jnp.zeros((rest, out_ref.shape[1]), jnp.float32)


def first_kernel(sums_ref, next_ref, gram_ref):
    blocks, vectors, _ = next_ref.shape
    height = vectors + vectors // 2
    grams = [unpacked(sums_ref[b * height + vectors : (b + 1) * height]) for b in range(blocks)]
    factors = factor(grams)
    for b in range(blocks):
        image = product(factors[b][0], sums_ref[b * height : b * height + vectors], 0)
        next_ref[b] = image
        gram_ref[b] = quadrants(product(image, image, 1))


def second_kernel(owner_ref, index_ref, image_ref, grams_ref, basis_ref, eigen_ref, owned_ref):
    blocks, vectors, slab_rows = image_ref.shape
    root_scale = math.sqrt(grams_ref.shape[0] * slab_rows)
    grams = []
    for b in range(blocks):
        rows = grams_ref[0, b]
        for t in range(1, grams_ref.shape[0]):
            rows = rows + grams_ref[t, b]
        grams.append(whole_gram(rows, vectors))
    factors = factor(grams)
    owned = [jnp.zeros((1, vectors), jnp.float32) for _ in range(CAP)]
    for b in range(blocks):
        basis_ref[b] = product(factors[b][0], image_ref[b], 0) * root_scale
        eigen_ref[b : b + 1] = factors[b][1]
        slot = jnp.int32(0)
        for earlier in range(b):
            slot = slot + jnp.where(owner_ref[earlier] == owner_ref[b], 1, 0)
        mine = owner_ref[b] == index_ref[0]
        for s in range(CAP):
            owned[s] = owned[s] + jnp.where(mine & (slot == s), factors[b][1], 0.0)
    for s in range(CAP):
        owned_ref[s : s + 1] = owned[s]


def copies(x, n):
    return jnp.broadcast_to(x[None], (n,) + x.shape)


def f32(*dims):
    return jax.ShapeDtypeStruct(dims, jnp.float32)


def body(activations, basis_init, owner_table):
    dp_count = lax.axis_size("dp")
    tp_count = lax.axis_size("tensor")
    dp_index = lax.axis_index("dp")
    tp_index = lax.axis_index("tensor")
    tok_rows = activations.shape[0]
    blocks, slab_rows, vectors = basis_init.shape
    order_size = activations.shape[1] // blocks
    share = order_size // dp_count
    pairs = dp_count // 2

    halves = pl.BlockSpec((pairs, 1, share, slab_rows), lambda b, at, core: (0, b, 0, 0))
    keep, send = pl.pallas_call(
        functools.partial(cov_kernel, 1.0 / (tok_rows * dp_count)),
        grid_spec=pltpu.PrefetchScalarGridSpec(
            num_scalar_prefetch=2,
            grid=(blocks,),
            in_specs=[
                pl.BlockSpec((tok_rows, slab_rows), lambda b, at, core: (0, b * tp_count + at[0])),
                pl.BlockSpec((tok_rows, order_size), lambda b, at, core: (0, b)),
            ],
            out_specs=(halves, halves),
        ),
        out_shape=(f32(pairs, blocks, share, slab_rows),) * 2,
        name="cov",
        compiler_params=SMALL,
    )(jnp.reshape(tp_index, (1,)), jnp.reshape(dp_index & 1, (1,)), activations, activations)
    other_core = [(i, i ^ 1) for i in range(dp_count)]
    partner = lax.ppermute(send, "dp", other_core)
    same_core = [list(range(core, dp_count, 2)) for core in range(2)]
    pieces = lax.all_to_all(keep + partner, "dp", 0, 0, axis_index_groups=same_core)
    lanes = -(-blocks * vectors // 128) * 128
    piece = f32(blocks, share, slab_rows)
    cov_out, own, part = pl.pallas_call(
        piece_kernel, out_shape=(piece, piece, f32(share, lanes)), name="piece", compiler_params=SMALL
    )(pieces, jnp.swapaxes(basis_init, 1, 2))

    parts = lax.all_to_all(copies(part, tp_count), "tensor", 0, 0)
    height = vectors + vectors // 2
    each = -(-blocks * height // pairs)
    terms = pl.pallas_call(
        functools.partial(image_kernel, vectors), out_shape=f32(each * pairs, slab_rows), name="image", compiler_params=SMALL
    )(parts, own)
    terms = lax.all_to_all(terms.reshape(pairs, each * slab_rows), "dp", 0, 0, axis_index_groups=same_core)
    terms = jnp.sum(terms, axis=0)
    terms = terms + lax.ppermute(terms, "dp", other_core)
    sums = lax.all_to_all(copies(terms, pairs), "dp", 0, 0, axis_index_groups=same_core)
    sums = sums.reshape(each * pairs, slab_rows)

    image, gram = pl.pallas_call(
        first_kernel, out_shape=(f32(blocks, vectors, slab_rows), f32(blocks, 24, 128)), name="first", compiler_params=SMALL
    )(sums)
    grams = lax.all_to_all(copies(gram, tp_count), "tensor", 0, 0)
    scalars = pl.BlockSpec(memory_space=pltpu.SMEM)
    whole = pl.BlockSpec(memory_space=pltpu.VMEM)
    basis, eigen, owned = pl.pallas_call(
        second_kernel,
        in_specs=[scalars, scalars, whole, whole],
        out_shape=(f32(blocks, vectors, slab_rows), f32(blocks, vectors), f32(CAP, vectors)),
        name="second",
        compiler_params=SMALL,
    )(owner_table, jnp.reshape(dp_index, (1,)), image, grams)
    return (jnp.swapaxes(cov_out, 1, 2), jnp.swapaxes(basis, 1, 2), eigen, owned)


def solution(mesh):
    return jax.shard_map(
        body,
        mesh=mesh,
        in_specs=(P("dp", None), P(None, "tensor", None), P()),
        out_specs=(P(None, "tensor", "dp"), P(None, "tensor", None), P(), P("dp", None)),
        check_vma=False,
    )
```
